32 devices in a mesh: parts: 2 (over y), dp: 4 (over z), mp: 2 (over x), rep: 2 (over core).
Axes of the slice: x: 2, y: 2, z: 4, core: 2. Of those that a mesh axis runs over, the one named last changes fastest.
Arguments:
- hidden_in: bfloat16 [64, 256, 1024], P(('parts', 'dp', 'rep')), parts along dimension 0, may hold values from -6 to 6
- doc_lengths: int32 [64], P(('parts', 'dp', 'rep')), parts along dimension 0, may hold values from 32 to 256
- w_qkv: bfloat16 [1024, 3, 1024], P('dp', None, 'mp'), may hold values from -6 to 6
- w_out: bfloat16 [1024, 1024], P('mp', 'dp'), may hold values from -0.1875 to 0.1875
- w_up: bfloat16 [1024, 4096], P('dp', 'mp'), may hold values from -0.1875 to 0.1875
- w_down: bfloat16 [4096, 1024], P('mp', 'dp'), may hold values from -0.09375 to 0.09375
- stored_embed: bfloat16 [2016, 1024], P(('parts', 'dp', 'mp', 'rep')), parts along dimension 0, may hold values from -6 to 6
- doc_labels: int32 [2080, 1], P(('parts', 'dp', 'mp', 'rep')), parts along dimension 0, may hold values from 0 to 3; in each aligned block of 65 rows (0 to 64, 65 to 129, ...) at most 26 rows name the same one
- doc_order: int32 [2080], P(('parts', 'dp', 'mp', 'rep')), parts along dimension 0, may hold values from 0 to 1039, each once
Outputs:
- best: float32 [2080], P(('parts', 'dp', 'mp', 'rep')), parts along dimension 0
The draws below stay inside these ranges and needn't reach their ends.
There are 2 independent parts, one for each index of `parts`. The reference program is written for one: setup_inputs(seed, part) draws one part's arguments, and reference() takes and returns one part's arrays. A program takes and returns all parts, laid end to end along the dimension named above; an argument that names none is the same for every part. Nothing has to cross between parts.
Inputs may be any that keep to these rules, and one draw needn't show every extreme that they name: `doc_labels`: no label appears on more than 26 of the rows of one device. `doc_order`: every rank appears once.
All inputs are finite; a program needn't handle non-finite values.
Results may differ from the reference program's by a relative error of at most 0.005.
Values may be sent and summed in bfloat16 or wider, within the bound.
No kernel may reach another device: no remote copies, remote signals or barrier semaphores. Data moves between devices by JAX's collectives and lax.ppermute only.
A program may use at most 64 MiB of HBM per device.

```python
import math
import jax
import jax.numpy as jnp
import numpy as np
from jax import lax

D = 1024
HEADS = 16
HEAD = 64
FF = 4096
SEQ = 256
DOC_DEV = 4
STORE = 63
DOCS = 32
ROWS = 65
STORED = 1008
ALLDOCS = 1040
CLUSTERS = 4
CAP = 26
N_DP = 4
N_MP = 2
N_REP = 2


def draw_w_qkv(key, part):
    first = jax.random.fold_in(key, 0)
    base = jnp.clip(jax.random.normal(first, (D, 3, D), jnp.float32), -6.0, 6.0) * D ** (-0.5)
    return base.astype(jnp.bfloat16)


def with_ends(values, rng, least, top_value):
    extent = values.shape
    index_at = [jax.random.randint(jax.random.fold_in(rng, axis), (), 0, extent[axis]) for axis in range(len(extent))]
    values = values.at[tuple(index_at)].set(least)
    longest = extent.index(max(extent))
    index_at[longest] = (index_at[longest] + 1) % extent[longest]
    return values.at[tuple(index_at)].set(top_value)


def level_of(rng, shape, pieces, least, high):
    gain, own = 1.0, jax.random.fold_in(rng, 6)
    for dim, blocks in pieces:
        heights = jnp.exp(jax.random.uniform(jax.random.fold_in(own, dim), (blocks,), jnp.float32, least / len(pieces), high / len(pieces)))
        gain = gain * jnp.repeat(heights, shape[dim] // blocks).reshape([-1 if axis == dim else 1 for axis in range(len(shape))])
    return gain


def deal_out(own_key, own, number, rows, number_of, top, bound, lean):
    ranking = jax.random.permutation(own_key, number_of)
    crowded, common = portions_of(number_of, rows * top, bound, lean, True), portions_of(number_of, rows * top, bound, lean, False)
    places = jnp.arange(number_of)

    def named(lengths, rotation):
        used = int((lengths > 0).sum())
        fixed = max(1, used // 4)
        shifted = fixed + (places - fixed + rotation * (used - fixed)) % max(1, number_of - fixed)
        return jnp.zeros((number_of,), jnp.int32).at[ranking[jnp.where(places < fixed, places, shifted)]].set(jnp.asarray(lengths, jnp.int32))

    lengths = jnp.where(number % 4 == 0, named(crowded, number // 4), named(common, number - number // 4 - 1))
    mixed = jax.random.permutation(jax.random.fold_in(own, 3), number_of)
    donor, sink = mixed[0:number_of // 2 * 2:2], mixed[1:number_of // 2 * 2:2]
    slack = jnp.minimum(lengths[donor] - 1, bound - lengths[sink]) // 2
    slack = jnp.where((donor == ranking[0]) | (sink == ranking[0]) | (lengths[sink] == 0), 0, jnp.maximum(slack, 0))
    shifted = jax.random.randint(jax.random.fold_in(own, 4), (number_of // 2,), 0, 1 << 20) % (slack + 1)
    lengths = lengths.at[donor].add(-shifted).at[sink].add(shifted)
    items = jnp.searchsorted(jnp.cumsum(lengths), jnp.arange(rows * top), side="right").astype(jnp.int32)
    listing = items.reshape(top, rows).T
    listing = listing[jax.random.permutation(jax.random.fold_in(own, 1), rows)]
    rotation = jax.random.randint(jax.random.fold_in(own, 2), (rows, 1), 0, top)
    return jnp.take_along_axis(listing, (jnp.arange(top)[None, :] + rotation) % top, axis=1)


def portions_of(amount, total, limit, slope, full):
    portions = [(1 << 20) // math.isqrt(standing ** slope) + 1 for standing in range(1, amount + 1)]
    largest = limit if full else min(limit, max(-(-total // amount), total * portions[0] // sum(portions)))
    least = 1 if total - largest >= amount - 1 else 0
    holding, surplus = [largest] + [least] * (amount - 1), total - largest - least * (amount - 1)
    while surplus > 0:
        candidates = [i for i in range(1, amount) if holding[i] < largest] or [i for i in range(1, amount) if holding[i] < limit]
        pool, left = sum([portions[i] for i in candidates]), surplus
        for i in candidates:
            more = min(limit - holding[i], max(1, left * portions[i] // pool), surplus)
            holding[i] = holding[i] + more
            surplus = surplus - more
    return np.array(holding)


def bell_draw(own_key, extent, scale, most, cuts=(), kind=jnp.bfloat16):
    array = scale * jax.random.normal(own_key, extent, jnp.float32)
    if cuts:
        array = array * level_of(own_key, extent, cuts, -0.22, 0.18)
    return jnp.clip(array, -most, most).astype(kind)


def setup_inputs(seed: int = 0, part: int = 0) -> dict:
    seeds = jax.random.split(jax.random.key(seed), 10)
    part_splits = jax.random.split(jax.random.fold_in(seeds[9], part), 10)
    hidden_in = bell_draw(part_splits[0], (DOCS, SEQ, D), 1.0, 6.0, ((0, 8),))
    doc_lengths = with_ends(jax.random.randint(part_splits[1], (DOCS,), SEQ // 8, SEQ + 1), jax.random.fold_in(part_splits[1], 1), SEQ // 8, SEQ).astype(jnp.int32)
    w_qkv = draw_w_qkv(jax.random.fold_in(seeds[9], 71), part)
    w_out = bell_draw(seeds[3], (D, D), D ** -0.5, 0.1875, ((0, 2), (1, 4)))
    w_up = bell_draw(seeds[4], (D, FF), D ** -0.5, 0.1875, ((0, 4), (1, 2)))
    w_down = bell_draw(seeds[5], (FF, D), FF ** -0.5, 0.09375, ((0, 2), (1, 4)))
    stored_embed = bell_draw(part_splits[6], (STORED, D), 1.0, 6.0, ((0, 16),))
    doc_labels_keys = jax.random.split(jax.random.fold_in(part_splits[7], 1), ALLDOCS // ROWS)
    doc_labels_turns = jax.random.permutation(jax.random.fold_in(part_splits[7], 3), ALLDOCS // ROWS)
    doc_labels = jax.vmap(lambda own, number: deal_out(jax.random.fold_in(part_splits[7], 2), own, number, ROWS, CLUSTERS, 1, CAP, 2))(doc_labels_keys, doc_labels_turns).reshape((ALLDOCS, 1))
    doc_order = jax.random.permutation(part_splits[8], ALLDOCS).astype(jnp.int32)
    return {"hidden_in": hidden_in, "doc_lengths": doc_lengths, "w_qkv": w_qkv, "w_out": w_out, "w_up": w_up, "w_down": w_down, "stored_embed": stored_embed, "doc_labels": doc_labels, "doc_order": doc_order}


def normalize(values):
    centred = values - lax.optimization_barrier(jnp.mean(values, axis=-1, keepdims=True))
    spread = lax.optimization_barrier(jnp.mean(centred * centred, axis=-1, keepdims=True))
    return centred * lax.rsqrt(spread + 1e-05)

def unit_rows(values):
    return (values * lax.rsqrt(lax.optimization_barrier(jnp.sum(values * values, axis=-1, keepdims=True)) + 1e-06)).astype(jnp.bfloat16)

def encode_one(hidden, length, w_qkv, w_out, w_up, w_down):
    residual = hidden.astype(jnp.float32)
    normed = normalize(residual).astype(jnp.bfloat16)
    projected = jnp.einsum('sd,dte->ste', normed.astype(jnp.float32), w_qkv.astype(jnp.float32)).astype(jnp.bfloat16)
    stacked = projected.reshape(SEQ, 3, HEADS, HEAD)
    queries = stacked[:, 0].astype(jnp.float32)
    key_heads = stacked[:, 1].astype(jnp.float32)
    values = stacked[:, 2].astype(jnp.float32)
    scores = jnp.einsum('qhe,khe->hqk', queries, key_heads) * HEAD ** (-0.5)
    positions = jnp.arange(SEQ, dtype=jnp.int32)
    key_valid = positions < length
    scores = jnp.where(key_valid[None, None, :], scores, -jnp.inf)
    attention = jax.nn.softmax(scores, axis=-1).astype(jnp.bfloat16)
    context = jnp.einsum('hqk,khe->qhe', attention.astype(jnp.float32), values).astype(jnp.bfloat16)
    context = context.reshape(SEQ, N_MP, D // N_MP).astype(jnp.float32)
    grouped = jnp.einsum('sgf,gfd->gsd', context, w_out.reshape(N_MP, D // N_MP, D).astype(jnp.float32))
    rounded = lax.optimization_barrier(grouped.astype(jnp.bfloat16))
    residual = residual + lax.optimization_barrier(jnp.sum(rounded.astype(jnp.float32), axis=0))
    hidden_normed = normalize(residual).astype(jnp.bfloat16)
    activated = jax.nn.gelu(jnp.dot(hidden_normed, w_up, preferred_element_type=jnp.float32), approximate=False).astype(jnp.bfloat16)
    mlp_out = jnp.dot(activated, w_down, preferred_element_type=jnp.float32)
    valid = key_valid.astype(jnp.float32)
    return lax.optimization_barrier(jnp.sum(valid[:, None] * (residual + mlp_out), axis=0)) / length.astype(jnp.float32)

def reference(hidden_in, doc_lengths, w_qkv, w_out, w_up, w_down, stored_embed, doc_labels, doc_order):

    def encode_item(item):
        return encode_one(item[0], item[1], w_qkv, w_out, w_up, w_down)
    pooled = lax.map(encode_item, (hidden_in, doc_lengths))
    new_units = unit_rows(pooled)
    new_count = DOC_DEV // N_MP
    arranged = new_units.reshape(N_DP, N_REP, N_MP, new_count, D).transpose(0, 2, 1, 3, 4)
    stored_units = unit_rows(stored_embed.astype(jnp.float32)).reshape(N_DP, N_MP, N_REP, STORE, D)
    all_units = jnp.concatenate([arranged, stored_units], axis=3).reshape(-1, D)
    labels_flat = doc_labels[:, 0]

    def best_block(item):
        units, labels_here, order_here = item
        similar = jnp.dot(units, all_units.T, preferred_element_type=jnp.float32)
        earlier = (labels_flat[None, :] == labels_here[:, None]) & (doc_order[None, :] < order_here[:, None])
        largest = lax.optimization_barrier(jnp.max(jnp.where(earlier, similar, -2.0), axis=1))
        return jnp.where(largest < -1.5, 0.0, largest)
    best = lax.map(best_block, (all_units.reshape(-1, ROWS, D), labels_flat.reshape(-1, ROWS), doc_order.reshape(-1, ROWS)))
    return best.reshape(-1)
```

```python
import functools

import jax
import jax.numpy as jnp
from jax import lax
from jax.experimental import pallas as pl
from jax.experimental.pallas import tpu as pltpu
from jax.sharding import PartitionSpec as P

HEAD = 64
CL_OWN = 1
F32 = jnp.float32
BF16 = jnp.bfloat16
MB = 1 << 20


def normalize(values):
    centred = values - jnp.mean(values, axis=-1, keepdims=True)
    spread = jnp.mean(centred * centred, axis=-1, keepdims=True)
    return centred * lax.rsqrt(spread + 1e-05)


def unit_rows(values):
    return (values * lax.rsqrt(jnp.sum(values * values, axis=-1, keepdims=True) + 1e-06)).astype(
        jnp.bfloat16
    )


def shards(hidden_in, doc_lengths, w_qkv, w_out, w_up, w_down, stored_embed, doc_labels, doc_order):
    replica = lax.axis_index("rep")
    copies = lax.axis_size("rep")

    def rep_half(weight, along):
        extent = weight.shape[along] // copies
        return lax.dynamic_slice_in_dim(weight, replica * extent, extent, along)

    halves = (
        lax.all_gather(rep_half(w_qkv, 2), "dp", axis=0, tiled=True),
        lax.all_gather(rep_half(w_out, 0), "dp", axis=1, tiled=True),
        lax.all_gather(rep_half(w_up, 1), "dp", axis=0, tiled=True),
        lax.all_gather(rep_half(w_down, 0), "dp", axis=1, tiled=True),
    )
    qkv_full, out_full, up_full, down_full = (
        lax.all_gather(halves[0], "rep", axis=2, tiled=True),
        lax.all_gather(halves[1], "rep", axis=0, tiled=True),
        lax.all_gather(halves[2], "rep", axis=1, tiled=True),
        lax.all_gather(halves[3], "rep", axis=0, tiled=True),
    )
    doc_count, seq_len, _ = hidden_in.shape
    mp_index = lax.axis_index("mp")
    residual = hidden_in.astype(jnp.float32)
    normed = normalize(residual).astype(jnp.bfloat16)
    projected = jnp.einsum(
        "bsd,dte->bste", normed, qkv_full, preferred_element_type=jnp.float32
    ).astype(jnp.bfloat16)
    local_heads = qkv_full.shape[2] // HEAD
    stacked = projected.reshape(doc_count, seq_len, 3, local_heads, HEAD)
    queries = stacked[:, :, 0]
    key_heads = stacked[:, :, 1]
    values = stacked[:, :, 2]
    scores = jnp.einsum(
        "bqhe,bkhe->bhqk", queries, key_heads, preferred_element_type=jnp.float32
    ) * HEAD ** (-0.5)
    positions = jnp.arange(seq_len, dtype=jnp.int32)
    key_valid = positions[None, :] < doc_lengths[:, None]
    scores = jnp.where(key_valid[:, None, None, :], scores, -jnp.inf)
    attention = jax.nn.softmax(scores, axis=-1).astype(jnp.bfloat16)
    context = jnp.einsum(
        "bhqk,bkhe->bqhe", attention, values, preferred_element_type=jnp.float32
    ).astype(jnp.bfloat16)
    context = context.reshape(doc_count, seq_len, local_heads * HEAD)
    attn_part = jnp.einsum("bsf,fd->bsd", context, out_full, preferred_element_type=jnp.float32)
    residual = residual + lax.psum(attn_part.astype(jnp.bfloat16), "mp").astype(jnp.float32)
    hidden_normed = normalize(residual).astype(jnp.bfloat16)
    activated = jax.nn.gelu(
        jnp.einsum("bsd,df->bsf", hidden_normed, up_full, preferred_element_type=jnp.float32),
        approximate=False,
    ).astype(jnp.bfloat16)
    mlp_part = jnp.einsum("bsf,fd->bsd", activated, down_full, preferred_element_type=jnp.float32)
    valid = key_valid.astype(jnp.float32)
    pooled_part = jnp.sum(valid[:, :, None] * mlp_part, axis=1)
    pooled = lax.psum_scatter(pooled_part, "mp", scatter_dimension=0, tiled=True)
    new_count = pooled.shape[0]
    my_valid = lax.dynamic_slice_in_dim(valid, mp_index * new_count, new_count, 0)
    my_residual = lax.dynamic_slice_in_dim(residual, mp_index * new_count, new_count, 0)
    my_lengths = lax.dynamic_slice_in_dim(doc_lengths, mp_index * new_count, new_count, 0)
    pooled = (pooled + jnp.sum(my_valid[:, :, None] * my_residual, axis=1)) / my_lengths[
        :, None
    ].astype(jnp.float32)
    row_units = jnp.concatenate(
        [unit_rows(pooled), unit_rows(stored_embed.astype(jnp.float32))], axis=0
    )
    row_count = row_units.shape[0]
    clusters = CL_OWN * lax.axis_size("dp")
    capacity = (row_count + clusters - 1) // clusters + (row_count + 2 * clusters - 1) // (
        2 * clusters
    )
    labels_flat = doc_labels[:, 0]
    member = (labels_flat[:, None] == jnp.arange(clusters, dtype=jnp.int32)[None, :]).astype(
        jnp.int32
    )
    before = jnp.cumsum(member, axis=0) - member
    slot_index = jnp.sum(before * member, axis=1)
    target = labels_flat * capacity + slot_index
    placed = target[None, :] == jnp.arange(clusters * capacity, dtype=jnp.int32)[:, None]
    send_units = jnp.dot(
        placed.astype(jnp.bfloat16), row_units, preferred_element_type=jnp.float32
    ).astype(jnp.bfloat16)
    send_units = send_units.reshape(clusters, capacity, row_units.shape[1])
    send_order = (jnp.sum(jnp.where(placed, doc_order[None, :] + 1, 0), axis=1) - 1).reshape(
        clusters, capacity
    )
    owned_units, owned_order = (
        lax.all_to_all(send_units, "dp", split_axis=0, concat_axis=1, tiled=True),
        lax.all_to_all(send_order, "dp", split_axis=0, concat_axis=1, tiled=True),
    )
    block_units, block_order = (
        lax.all_gather(owned_units, ("mp", "rep"), axis=1, tiled=True),
        lax.all_gather(owned_order, ("mp", "rep"), axis=1, tiled=True),
    )
    similar = jnp.einsum(
        "cqd,ckd->cqk", owned_units, block_units, preferred_element_type=jnp.float32
    )
    earlier = (block_order[:, None, :] >= 0) & (block_order[:, None, :] < owned_order[:, :, None])
    largest = jnp.max(jnp.where(earlier, similar, -2.0), axis=2)
    best_slot = jnp.where(largest < -1.5, 0.0, largest)
    returned = lax.all_to_all(best_slot, "dp", split_axis=1, concat_axis=0, tiled=True)
    return jnp.sum(jnp.where(placed, returned.reshape(-1)[:, None], 0.0), axis=0)


def swap(value, axis, bit=1):
    count = lax.axis_size(axis)
    return lax.ppermute(value, axis, [(i, i ^ bit) for i in range(count)])


def doubled(value, axis):
    bit = 1
    while bit < lax.axis_size(axis):
        value = jnp.concatenate([value, swap(value, axis, bit)], axis=0)
        bit *= 2
    return value


def quarter_index(step):
    return (lax.axis_index("parts") ^ (step >> 1)) * 2 + (lax.axis_index("rep") ^ (step & 1))


def block_at(step, size):
    return pl.ds(pl.multiple_of((lax.axis_index("dp") ^ step) * size, size), size)


def whole(array):
    zeros = (0,) * array.ndim
    return pl.BlockSpec(array.shape, lambda *_: zeros)


def call(body, grid, operands, specs, out_shape, out_specs, scratch, cost, vmem, lengths):
    return pl.pallas_call(
        body,
        out_shape=out_shape,
        grid_spec=pltpu.PrefetchScalarGridSpec(
            num_scalar_prefetch=1,
            grid=grid,
            in_specs=specs,
            out_specs=out_specs,
            scratch_shapes=scratch,
        ),
        compiler_params=pltpu.CompilerParams(vmem_limit_bytes=vmem * MB),
        cost_estimate=pl.CostEstimate(flops=cost, bytes_accessed=4 * MB, transcendentals=0),
    )(lengths, *operands)


def attention_body(step, pieces, lengths, normed, local, *refs):
    remote, out = refs[:-1], refs[-1]
    length = lengths[pl.program_id(0)]
    width = out.shape[1]
    depth = local.shape[1]
    at = pl.ds(pl.multiple_of(quarter_index(step) * width, width), width)
    joined = jnp.concatenate([local[t, :, at] for t in range(3)], axis=1)
    total = jnp.dot(normed[:, block_at(0, depth)], joined, preferred_element_type=F32)
    for e in range(1, pieces):
        piece = remote[e - 1]
        joined = jnp.concatenate([piece[t] for t in range(3)], axis=1)
        total += jnp.dot(normed[:, block_at(e, depth)], joined, preferred_element_type=F32)
    projected = total.astype(BF16)
    queries, keys, values = (projected[:, t * width : (t + 1) * width] for t in range(3))
    seq = queries.shape[0]
    lane = lax.broadcasted_iota(jnp.int32, (seq, width), 1)
    valid = lax.broadcasted_iota(jnp.int32, (seq, seq), 1) < length
    context = jnp.zeros((seq, width), F32)
    for head in range(width // HEAD):
        mine = (lane >= head * HEAD) & (lane < (head + 1) * HEAD)
        scores = lax.dot_general(
            jnp.where(mine, queries, jnp.zeros_like(queries)),
            keys,
            (((1,), (1,)), ((), ())),
            preferred_element_type=F32,
        ) * HEAD ** (-0.5)
        scores = jnp.where(valid, scores, -jnp.inf)
        top = jnp.max(scores, axis=1, keepdims=True)
        weight = jnp.exp(scores - top)
        weight = weight * (1.0 / jnp.sum(weight, axis=1, keepdims=True))
        got = jnp.dot(weight.astype(BF16), values, preferred_element_type=F32)
        context = jnp.where(mine, got, context)
    out[...] = context.astype(BF16)


def attention_call(step, normed, local, remote, lengths, seq):
    rows, features = normed.shape
    width = remote[0].shape[2]
    return call(
        functools.partial(attention_body, step, len(remote) + 1),
        (rows // seq,),
        [normed, local, *remote],
        [pl.BlockSpec((seq, features), lambda i, _: (i, 0)), whole(local), *map(whole, remote)],
        jax.ShapeDtypeStruct((rows, width), BF16),
        pl.BlockSpec((seq, width), lambda i, _: (i, 0)),
        [],
        2 * rows * features * width * 3 + 8 * rows * seq * width,
        20,
        lengths,
    )


def out_body(pieces, lengths, hidden, out_local, out_peer, *refs):
    own, peer = refs[:4], refs[4:8]
    packed = refs[8 : 8 + 4 * (pieces - 1)]
    hidden_normed, pooled, total = refs[8 + 4 * (pieces - 1) :]
    length = lengths[pl.program_id(0)]
    width = own[0].shape[1]
    depth = out_local.shape[1]
    context = jnp.concatenate([ref[...] for ref in own + peer], axis=1)
    rows = [pl.ds(pl.multiple_of(quarter_index(j) * width, width), width) for j in range(4)]
    weight = jnp.concatenate(
        [out_local[at, :] for at in rows] + [out_peer[at, :] for at in rows], axis=0
    )
    total[:, block_at(0, depth)] = jnp.dot(context, weight, preferred_element_type=F32)
    for e in range(1, pieces):
        refs_e = [packed[j * (pieces - 1) + e - 1] for j in range(4)]
        weight = jnp.concatenate(
            [ref[:width, :depth] for ref in refs_e] + [ref[:width, depth:] for ref in refs_e],
            axis=0,
        )
        total[:, block_at(e, depth)] = jnp.dot(context, weight, preferred_element_type=F32)
    residual = total[...] + hidden[...].astype(F32)
    hidden_normed[...] = normalize(residual).astype(BF16)
    seq = residual.shape[0]
    valid = lax.broadcasted_iota(jnp.int32, residual.shape, 0) < length
    summed = jnp.sum(jnp.where(valid, residual, 0.0), axis=0, keepdims=True)
    pooled[...] = jnp.broadcast_to(summed, pooled.shape)


def out_call(hidden, out_local, out_peer, own, peer, packed, lengths, seq):
    rows, features = hidden.shape
    width = own[0].shape[1]
    flat = [piece for group in packed for piece in group]
    row_spec = pl.BlockSpec((seq, features), lambda i, _: (i, 0))
    context_spec = pl.BlockSpec((seq, width), lambda i, _: (i, 0))
    return call(
        functools.partial(out_body, len(packed[0]) + 1),
        (rows // seq,),
        [hidden, out_local, out_peer, *own, *peer, *flat],
        [row_spec, whole(out_local), whole(out_peer)] + [context_spec] * 8 + [*map(whole, flat)],
        (
            jax.ShapeDtypeStruct((rows, features), BF16),
            jax.ShapeDtypeStruct((8 * (rows // seq), features), F32),
        ),
        (row_spec, pl.BlockSpec((8, features), lambda i, _: (i, 0))),
        [pltpu.VMEM((seq, features), F32)],
        2 * rows * features * features,
        32,
        lengths,
    )


def up_body(step, pieces, lengths, hidden_normed, local, *refs):
    remote, out = refs[:-1], refs[-1]
    length = lengths[pl.program_id(0)]
    width = out.shape[1]
    depth = local.shape[0]
    at = pl.ds(pl.multiple_of(quarter_index(step) * width, width), width)
    total = jnp.dot(hidden_normed[:, block_at(0, depth)], local[:, at], preferred_element_type=F32)
    for e in range(1, pieces):
        piece = remote[e - 1]
        skip = piece.shape[0] - depth
        total += jnp.dot(
            hidden_normed[:, block_at(e, depth)], piece[skip:, :], preferred_element_type=F32
        )
    active = 0.5 * total * (1.0 + lax.erf(total * 0.5**0.5))
    valid = lax.broadcasted_iota(jnp.int32, total.shape, 0) < length
    active = jnp.where(valid, active.astype(BF16).astype(F32), 0.0)
    out[...] = jnp.broadcast_to(jnp.sum(active, axis=0, keepdims=True), out.shape)


def up_call(step, hidden_normed, local, remote, lengths, seq):
    rows, features = hidden_normed.shape
    width = remote[0].shape[1]
    return call(
        functools.partial(up_body, step, len(remote) + 1),
        (rows // seq,),
        [hidden_normed, local, *remote],
        [pl.BlockSpec((seq, features), lambda i, _: (i, 0)), whole(local), *map(whole, remote)],
        jax.ShapeDtypeStruct((8 * (rows // seq), width), F32),
        pl.BlockSpec((8, width), lambda i, _: (i, 0)),
        [],
        2 * rows * features * width,
        24,
        lengths,
    )


def fast(hidden_in, doc_lengths, w_qkv, w_out, w_up, w_down, stored_embed, doc_labels, doc_order):
    docs, seq, features = hidden_in.shape
    n_dp, n_mp = lax.axis_size("dp"), lax.axis_size("mp")
    m, z = lax.axis_index("mp"), lax.axis_index("dp")
    depth = w_qkv.shape[0]
    rows = docs * seq
    quarter = quarter_index(0)
    spans = range(1, n_dp)

    qkv_local = jnp.transpose(w_qkv, (1, 0, 2))
    width = qkv_local.shape[2] // 4
    piece = lax.dynamic_slice_in_dim(qkv_local, quarter * width, width, 2)
    qkv = [[swap(piece, "dp", e) for e in spans]]
    out_peer = swap(w_out, "mp")
    qkv.append([swap(p, "rep") for p in qkv[0]])
    qkv.append([swap(p, "parts") for p in qkv[0]])
    qkv.append([swap(p, "rep") for p in qkv[2]])

    out_rows, up_width = w_out.shape[0] // 4, w_up.shape[1] // 4
    packed = jnp.concatenate(
        [
            jnp.concatenate(
                [
                    lax.dynamic_slice_in_dim(w, quarter * out_rows, out_rows, 0)
                    for w in (w_out, out_peer)
                ],
                axis=1,
            ),
            lax.dynamic_slice_in_dim(w_up, quarter * up_width, up_width, 1),
        ],
        axis=0,
    )
    packed, *held = lax.optimization_barrier((packed, *qkv[0]))
    rest = [[swap(packed, "dp", e) for e in spans]]
    rest.append([swap(p, "rep") for p in rest[0]])
    rest.append([swap(p, "parts") for p in rest[0]])
    rest.append([swap(p, "rep") for p in rest[2]])

    hidden = hidden_in.reshape(rows, features)
    normed = normalize(hidden.astype(F32)).astype(BF16)
    own = [
        attention_call(j, normed, qkv_local, qkv[j], doc_lengths, seq) for j in range(4)
    ]
    peer = [swap(c, "mp") for c in own]
    hidden_normed, pooled_rows = out_call(
        hidden, w_out, out_peer, own, peer, rest, doc_lengths, seq
    )
    sums = [up_call(j, hidden_normed, w_up, rest[j], doc_lengths, seq) for j in range(4)]

    stored = stored_embed.shape[0]
    new = docs // n_mp
    labels = doc_labels[:, 0]

    def meta(values, filler):
        laid = jnp.concatenate(
            [values[new:], jnp.full((64 - stored,), filler, jnp.int32), values[:new]]
        )
        return jnp.pad(laid, (0, 128 - laid.shape[0]))

    label_row = meta(labels, -1)
    order_row = meta(doc_order, 0)
    last = jnp.concatenate([label_row, order_row // 128, order_row % 128])
    last = jnp.pad(last, (0, features - last.shape[0])).astype(BF16)
    block = jnp.concatenate([unit_rows(stored_embed.astype(F32)), last[None, :]], axis=0)
    block = block[None]
    every = doubled(doubled(doubled(block, "dp"), "mp"), "rep")
    blocks = every.shape[0]
    info = every[:, stored, :384].astype(jnp.int32)
    key_label, key_high, key_low = (info[:, t * 128 : t * 128 + 64].reshape(-1) for t in range(3))
    new_label, new_high, new_low = (
        info[:, t * 128 + 64 : t * 128 + 64 + new].reshape(-1) for t in range(3)
    )
    key_order = key_high * 128 + key_low
    new_order = new_high * 128 + new_low
    keys = every.reshape(blocks * 64, features)

    def largest_of(units, unit_label, unit_order, others, other_label, other_order):
        similar = lax.dot_general(
            units, others, (((1,), (1,)), ((), ())), preferred_element_type=F32
        )
        earlier = (unit_label[:, None] == other_label[None, :]) & (
            other_order[None, :] < unit_order[:, None]
        )
        return jnp.max(jnp.where(earlier, similar, -2.0), axis=1)

    stored_units = block[0, :stored]
    best_stored = largest_of(
        stored_units, labels[new:], doc_order[new:], keys, key_label, key_order
    )

    per_len = doc_lengths.astype(F32)[:, None]
    order = [quarter_index(j) for j in range(4)]
    summed = jnp.zeros((docs, w_up.shape[1]), F32)
    for j in range(4):
        summed = lax.dynamic_update_slice_in_dim(
            summed, sums[j][::8], order[j] * up_width, 1
        )
    pooled_rows = pooled_rows[::8]
    send = jnp.concatenate([summed, pooled_rows], axis=1) / per_len
    got = doubled(send, "dp")
    hid = got[:, : w_up.shape[1]]
    high = hid.astype(BF16)
    low = (hid - high.astype(F32)).astype(BF16)
    part = jnp.dot(high, w_down, preferred_element_type=F32) + jnp.dot(
        low, w_down, preferred_element_type=F32
    )
    mine = lax.dynamic_slice_in_dim(got, w_up.shape[1] + z * depth, depth, 1)
    part = part + jnp.where(m == 0, mine, 0.0)
    part = part + swap(part, "mp")
    rel = part.reshape(n_dp, docs, depth)
    lead = jnp.stack([lax.dynamic_index_in_dim(rel, z ^ e, 0, False) for e in range(n_dp)])
    cols = doubled(lead.reshape(1, n_dp * docs, depth), "dp")
    cols = jnp.stack([lax.dynamic_index_in_dim(cols, z ^ e, 0, False) for e in range(n_dp)], axis=1)
    pooled = cols.reshape(n_dp, docs, features)
    pooled = doubled(pooled[None], "rep")
    new_units = unit_rows(pooled).reshape(2, n_dp, n_mp, new, features)
    new_units = jnp.stack(
        [
            lax.dynamic_index_in_dim(
                lax.dynamic_index_in_dim(new_units, z ^ e, 1, False), m ^ f, 1, False
            )
            for f in range(n_mp)
            for e in range(n_dp)
        ],
        axis=1,
    )
    new_units = new_units.reshape(blocks * new, features)
    best_stored = jnp.maximum(
        best_stored,
        largest_of(stored_units, labels[new:], doc_order[new:], new_units, new_label, new_order),
    )
    best_new = jnp.maximum(
        largest_of(new_units[:new], labels[:new], doc_order[:new], keys, key_label, key_order),
        largest_of(new_units[:new], labels[:new], doc_order[:new], new_units, new_label, new_order),
    )
    best = jnp.concatenate([best_new, best_stored])
    return jnp.where(best < -1.5, 0.0, best)


def fits(mesh, hidden_in, w_qkv, w_out, w_up, stored_embed):
    size = mesh.shape
    depth = w_qkv.shape[0] // size["dp"]
    blocks = size["dp"] * size["mp"] * size["rep"] * size["parts"]
    return (
        size["parts"] == 2
        and size["rep"] == 2
        and size["mp"] == 2
        and size["dp"] == 4
        and depth % 128 == 0
        and w_qkv.shape[2] % (size["mp"] * 4 * 128) == 0
        and w_up.shape[1] % (size["mp"] * 4 * 128) == 0
        and size["mp"] * depth == w_up.shape[1] // (size["mp"] * 4)
        and hidden_in.shape[1] % 128 == 0
        and stored_embed.shape[0] // blocks == 63
    )


def solution(mesh):
    placed = (
        P(("parts", "dp", "rep"), None, None),
        P(("parts", "dp", "rep")),
        P("dp", None, "mp"),
        P("mp", "dp"),
        P("dp", "mp"),
        P("mp", "dp"),
        P(("parts", "dp", "mp", "rep"), None),
        P(("parts", "dp", "mp", "rep"), None),
        P(("parts", "dp", "mp", "rep")),
    )

    def run(*arrays):
        hidden_in, _, w_qkv, w_out, w_up, _, stored_embed = arrays[:7]
        plan = fast if fits(mesh, hidden_in, w_qkv, w_out, w_up, stored_embed) else shards
        return jax.shard_map(
            plan,
            mesh=mesh,
            in_specs=placed,
            out_specs=P(("parts", "dp", "mp", "rep")),
            check_vma=False,
        )(*arrays)

    return run
```

```python
import functools

import jax
import jax.numpy as jnp
from jax import lax
from jax.experimental import pallas as pl
from jax.experimental.pallas import tpu as pltpu
from jax.sharding import PartitionSpec as P

HEAD = 64
CL_OWN = 1
F32 = jnp.float32
BF16 = jnp.bfloat16
MB = 1 << 20


def normalize(values):
    centred = values - jnp.mean(values, axis=-1, keepdims=True)
    spread = jnp.mean(centred * centred, axis=-1, keepdims=True)
    return centred * lax.rsqrt(spread + 1e-05)


def unit_rows(values):
    return (values * lax.rsqrt(jnp.sum(values * values, axis=-1, keepdims=True) + 1e-06)).astype(
        jnp.bfloat16
    )


def shards(hidden_in, doc_lengths, w_qkv, w_out, w_up, w_down, stored_embed, doc_labels, doc_order):
    replica = lax.axis_index("rep")
    copies = lax.axis_size("rep")

    def rep_half(weight, along):
        extent = weight.shape[along] // copies
        return lax.dynamic_slice_in_dim(weight, replica * extent, extent, along)

    halves = (
        lax.all_gather(rep_half(w_qkv, 2), "dp", axis=0, tiled=True),
        lax.all_gather(rep_half(w_out, 0), "dp", axis=1, tiled=True),
        lax.all_gather(rep_half(w_up, 1), "dp", axis=0, tiled=True),
        lax.all_gather(rep_half(w_down, 0), "dp", axis=1, tiled=True),
    )
    qkv_full, out_full, up_full, down_full = (
        lax.all_gather(halves[0], "rep", axis=2, tiled=True),
        lax.all_gather(halves[1], "rep", axis=0, tiled=True),
        lax.all_gather(halves[2], "rep", axis=1, tiled=True),
        lax.all_gather(halves[3], "rep", axis=0, tiled=True),
    )
    doc_count, seq_len, _ = hidden_in.shape
    mp_index = lax.axis_index("mp")
    residual = hidden_in.astype(jnp.float32)
    normed = normalize(residual).astype(jnp.bfloat16)
    projected = jnp.einsum(
        "bsd,dte->bste", normed, qkv_full, preferred_element_type=jnp.float32
    ).astype(jnp.bfloat16)
    local_heads = qkv_full.shape[2] // HEAD
    stacked = projected.reshape(doc_count, seq_len, 3, local_heads, HEAD)
    queries = stacked[:, :, 0]
    key_heads = stacked[:, :, 1]
    values = stacked[:, :, 2]
    scores = jnp.einsum(
        "bqhe,bkhe->bhqk", queries, key_heads, preferred_element_type=jnp.float32
    ) * HEAD ** (-0.5)
    positions = jnp.arange(seq_len, dtype=jnp.int32)
    key_valid = positions[None, :] < doc_lengths[:, None]
    scores = jnp.where(key_valid[:, None, None, :], scores, -jnp.inf)
    attention = jax.nn.softmax(scores, axis=-1).astype(jnp.bfloat16)
    context = jnp.einsum(
        "bhqk,bkhe->bqhe", attention, values, preferred_element_type=jnp.float32
    ).astype(jnp.bfloat16)
    context = context.reshape(doc_count, seq_len, local_heads * HEAD)
    attn_part = jnp.einsum("bsf,fd->bsd", context, out_full, preferred_element_type=jnp.float32)
    residual = residual + lax.psum(attn_part.astype(jnp.bfloat16), "mp").astype(jnp.float32)
    hidden_normed = normalize(residual).astype(jnp.bfloat16)
    activated = jax.nn.gelu(
        jnp.einsum("bsd,df->bsf", hidden_normed, up_full, preferred_element_type=jnp.float32),
        approximate=False,
    ).astype(jnp.bfloat16)
    mlp_part = jnp.einsum("bsf,fd->bsd", activated, down_full, preferred_element_type=jnp.float32)
    valid = key_valid.astype(jnp.float32)
    pooled_part = jnp.sum(valid[:, :, None] * mlp_part, axis=1)
    pooled = lax.psum_scatter(pooled_part, "mp", scatter_dimension=0, tiled=True)
    new_count = pooled.shape[0]
    my_valid = lax.dynamic_slice_in_dim(valid, mp_index * new_count, new_count, 0)
    my_residual = lax.dynamic_slice_in_dim(residual, mp_index * new_count, new_count, 0)
    my_lengths = lax.dynamic_slice_in_dim(doc_lengths, mp_index * new_count, new_count, 0)
    pooled = (pooled + jnp.sum(my_valid[:, :, None] * my_residual, axis=1)) / my_lengths[
        :, None
    ].astype(jnp.float32)
    row_units = jnp.concatenate(
        [unit_rows(pooled), unit_rows(stored_embed.astype(jnp.float32))], axis=0
    )
    row_count = row_units.shape[0]
    clusters = CL_OWN * lax.axis_size("dp")
    capacity = (row_count + clusters - 1) // clusters + (row_count + 2 * clusters - 1) // (
        2 * clusters
    )
    labels_flat = doc_labels[:, 0]
    member = (labels_flat[:, None] == jnp.arange(clusters, dtype=jnp.int32)[None, :]).astype(
        jnp.int32
    )
    before = jnp.cumsum(member, axis=0) - member
    slot_index = jnp.sum(before * member, axis=1)
    target = labels_flat * capacity + slot_index
    placed = target[None, :] == jnp.arange(clusters * capacity, dtype=jnp.int32)[:, None]
    send_units = jnp.dot(
        placed.astype(jnp.bfloat16), row_units, preferred_element_type=jnp.float32
    ).astype(jnp.bfloat16)
    send_units = send_units.reshape(clusters, capacity, row_units.shape[1])
    send_order = (jnp.sum(jnp.where(placed, doc_order[None, :] + 1, 0), axis=1) - 1).reshape(
        clusters, capacity
    )
    owned_units, owned_order = (
        lax.all_to_all(send_units, "dp", split_axis=0, concat_axis=1, tiled=True),
        lax.all_to_all(send_order, "dp", split_axis=0, concat_axis=1, tiled=True),
    )
    block_units, block_order = (
        lax.all_gather(owned_units, ("mp", "rep"), axis=1, tiled=True),
        lax.all_gather(owned_order, ("mp", "rep"), axis=1, tiled=True),
    )
    similar = jnp.einsum(
        "cqd,ckd->cqk", owned_units, block_units, preferred_element_type=jnp.float32
    )
    earlier = (block_order[:, None, :] >= 0) & (block_order[:, None, :] < owned_order[:, :, None])
    largest = jnp.max(jnp.where(earlier, similar, -2.0), axis=2)
    best_slot = jnp.where(largest < -1.5, 0.0, largest)
    returned = lax.all_to_all(best_slot, "dp", split_axis=1, concat_axis=0, tiled=True)
    return jnp.sum(jnp.where(placed, returned.reshape(-1)[:, None], 0.0), axis=0)


QUARTERS = 4


def swap(value, axis, bit=1):
    count = lax.axis_size(axis)
    return lax.ppermute(value, axis, [(i, i ^ bit) for i in range(count)])


def both_swapped(value):
    return lax.ppermute(value, ("mp", "rep"), [(i, i ^ 3) for i in range(4)])


def after(value, *others):
    return lax.optimization_barrier((value, *others))[0]


def along_dp(value):
    far = swap(value, "dp", 2)
    return [swap(value, "dp", 1), far, swap(far, "dp", 1)]


def quarter_index(step):
    return (lax.axis_index("parts") ^ (step >> 1)) * 2 + (lax.axis_index("rep") ^ (step & 1))


def block_at(step, size):
    return pl.ds(pl.multiple_of((lax.axis_index("dp") ^ step) * size, size), size)


def quarter_at(step, size):
    return pl.ds(pl.multiple_of(quarter_index(step) * size, size), size)


VMEM_SPEC = pl.BlockSpec(memory_space=pltpu.VMEM)
SMEM_SPEC = pl.BlockSpec(memory_space=pltpu.SMEM)


def call(body, operands, out_shape, scratch=(), flops=0, vmem=16, scalars=0):
    count = len(operands)
    return pl.pallas_call(
        body,
        out_shape=out_shape,
        in_specs=[SMEM_SPEC] * scalars + [VMEM_SPEC] * (count - scalars),
        out_specs=jax.tree.map(lambda _: VMEM_SPEC, out_shape),
        scratch_shapes=list(scratch),
        compiler_params=pltpu.CompilerParams(vmem_limit_bytes=vmem * MB),
        cost_estimate=pl.CostEstimate(flops=flops, bytes_accessed=2 * MB, transcendentals=0),
    )(*operands)


def attention_body(steps, docs, lengths, normed, local, *refs):
    *remote, out, weight, projected = refs
    depth = local.shape[1]
    width = out.shape[1] // len(steps)
    each = len(remote) // len(steps)
    for i, step in enumerate(steps):
        at = quarter_at(step, width)
        for t in range(3):
            columns = slice((3 * i + t) * width, (3 * i + t + 1) * width)
            weight[block_at(0, depth), columns] = local[t, :, at]
            for e in range(each):
                weight[block_at(e + 1, depth), columns] = remote[i * each + e][t]
    projected[...] = jnp.dot(normed[...], weight[...], preferred_element_type=F32).astype(BF16)
    seq = normed.shape[0] // docs
    first = lax.broadcasted_iota(jnp.int32, (seq, width), 1) < HEAD
    key_at = lax.broadcasted_iota(jnp.int32, (1, seq), 1)
    for doc in range(docs):
        bias = jnp.where(key_at < lengths[doc], 0.0, -jnp.inf)
        rows = slice(doc * seq, (doc + 1) * seq)
        for i in range(len(steps)):
            queries, keys, values = (
                projected[rows, (3 * i + t) * width : (3 * i + t + 1) * width] for t in range(3)
            )
            queries = queries * jnp.asarray(HEAD ** (-0.5), BF16)
            nothing = jnp.zeros_like(queries)
            pair = jnp.concatenate(
                [jnp.where(first, queries, nothing), jnp.where(first, nothing, queries)], axis=0
            )
            scores = lax.dot_general(
                pair, keys, (((1,), (1,)), ((), ())), preferred_element_type=F32
            )
            scores = scores + bias
            share = jnp.exp(scores - jnp.max(scores, axis=1, keepdims=True))
            scale = 1.0 / jnp.sum(share, axis=1, keepdims=True)
            got = jnp.dot(share.astype(BF16), values, preferred_element_type=F32) * scale
            out[rows, i * width : (i + 1) * width] = jnp.where(
                first, got[:seq], got[seq:]
            ).astype(BF16)


def attention_call(steps, normed, local, remote, lengths, docs):
    rows, features = normed.shape
    width = remote[0].shape[2] * len(steps)
    return call(
        functools.partial(attention_body, steps, docs),
        [lengths, normed, local, *remote],
        jax.ShapeDtypeStruct((rows, width), BF16),
        [pltpu.VMEM((features, 3 * width), BF16), pltpu.VMEM((rows, 3 * width), BF16)],
        flops=6 * rows * features * width,
        vmem=24,
        scalars=1,
    )


def out_body(docs, lengths, hidden, out_local, out_peer, *refs):
    contexts, pieces = refs[:4], refs[4:-4]
    hidden_normed, pooled, weight, total = refs[-4:]
    depth = out_local.shape[1]
    width = out_local.shape[0] // QUARTERS
    span = QUARTERS * width
    each = len(pieces) // 2
    for j in range(QUARTERS):
        at = quarter_at(j, width)
        rows, source = slice(j * width, (j + 1) * width), slice((j >> 1) * width, ((j >> 1) + 1) * width)
        peer_rows = slice(span + j * width, span + (j + 1) * width)
        weight[rows, block_at(0, depth)] = out_local[at, :]
        weight[peer_rows, block_at(0, depth)] = out_peer[at, :]
        for e in range(each):
            piece = pieces[(j & 1) * each + e]
            weight[rows, block_at(e + 1, depth)] = piece[source, :depth]
            weight[peer_rows, block_at(e + 1, depth)] = piece[source, depth:]
    half = hidden.shape[0] // 2
    seq = hidden.shape[0] // docs
    for i in range(2):
        rows = slice(i * half, (i + 1) * half)
        context = jnp.concatenate([ref[rows, :] for ref in contexts], axis=1)
        total[rows, :] = jnp.dot(context, weight[...], preferred_element_type=F32)
    for doc in range(docs):
        rows = slice(doc * seq, (doc + 1) * seq)
        residual = total[rows, :] + hidden[rows, :].astype(F32)
        hidden_normed[rows, :] = normalize(residual).astype(BF16)
        valid = lax.broadcasted_iota(jnp.int32, residual.shape, 0) < lengths[doc]
        pooled[doc : doc + 1, :] = jnp.sum(jnp.where(valid, residual, 0.0), axis=0, keepdims=True)


def out_call(hidden, out_local, out_peer, contexts, pieces, lengths, docs):
    rows, features = hidden.shape
    return call(
        functools.partial(out_body, docs),
        [lengths, hidden, out_local, out_peer, *contexts, *pieces],
        (
            jax.ShapeDtypeStruct((rows, features), BF16),
            jax.ShapeDtypeStruct((docs, features), F32),
        ),
        [pltpu.VMEM((features, features), BF16), pltpu.VMEM((rows, features), F32)],
        flops=2 * rows * features * features,
        vmem=28,
        scalars=1,
    )


def up_body(steps, docs, last, lengths, hidden_normed, local, *refs):
    out, weight = refs[-2:]
    remote = refs[: len(refs) - 2 - last]
    depth = local.shape[0]
    width = remote[0].shape[1]
    each = len(remote) // len(steps)
    for i, step in enumerate(steps):
        columns = slice(i * width, (i + 1) * width)
        weight[block_at(0, depth), columns] = local[:, quarter_at(step, width)]
        for e in range(each):
            weight[block_at(e + 1, depth), columns] = remote[i * each + e][...]
    half = hidden_normed.shape[0] // 2
    seq = hidden_normed.shape[0] // docs
    start = 0
    if last:
        sums, pooled = refs[len(remote) : len(remote) + 2]
        start = sums.shape[1]
        end = start + len(steps) * width
    for i in range(2):
        total = jnp.dot(
            hidden_normed[i * half : (i + 1) * half, :], weight[...], preferred_element_type=F32
        )
        active = 0.5 * total * (1.0 + lax.erf(total * 0.5**0.5))
        active = active.astype(BF16).astype(F32)
        for k in range(half // seq):
            doc = i * (half // seq) + k
            length = lengths[doc]
            part = active[k * seq : (k + 1) * seq, :]
            valid = lax.broadcasted_iota(jnp.int32, part.shape, 0) < length
            row = jnp.sum(jnp.where(valid, part, 0.0), axis=0, keepdims=True)
            at = slice(doc, doc + 1)
            if last:
                count = jnp.full((1, 1), length, jnp.int32).astype(F32)
                out[at, start:end] = row / count
                out[at, :start] = sums[at, :] / count
                out[at, end:] = pooled[at, :] / count
            else:
                out[at, :] = row


def up_call(steps, hidden_normed, local, remote, lengths, docs, others=()):
    rows, features = hidden_normed.shape
    width = remote[0].shape[1] * len(steps)
    return call(
        functools.partial(up_body, steps, docs, len(others)),
        [lengths, hidden_normed, local, *remote, *others],
        jax.ShapeDtypeStruct((docs, width + sum(o.shape[1] for o in others)), F32),
        [pltpu.VMEM((features, width), BF16)],
        flops=2 * rows * features * width,
        vmem=28,
        scalars=1,
    )


def down_body(*refs):
    *blocks, w_down, out, table = refs
    docs = blocks[0].shape[0]
    hidden, depth = w_down.shape
    width = hidden // QUARTERS
    for e, block in enumerate(blocks):
        table[e * docs : (e + 1) * docs, :] = block[...]
    sums = table[:, :hidden]
    high = sums.astype(BF16)
    low = (sums - high.astype(F32)).astype(BF16)
    both = jnp.concatenate([high, low], axis=0)
    total = jnp.zeros((both.shape[0], depth), F32)
    for j in range(QUARTERS):
        total += jnp.dot(
            both[:, j * width : (j + 1) * width],
            w_down[quarter_at(j, width), :],
            preferred_element_type=F32,
        )
    count = out.shape[0]
    start = pl.multiple_of(hidden + lax.axis_index("dp") * depth, depth)
    residual = table[:, pl.ds(start, depth)]
    first = (lax.axis_index("mp") == 0).astype(F32)
    out[...] = total[:count] + total[count:] + residual * first


def sum_body(own, over_mp, over_rep, over_both, out):
    count = own.shape[0]
    out[:count, :] = own[...] + over_mp[...]
    out[count:, :] = over_rep[...] + over_both[...]


def stored_body(new, blocks, labels, ranks, best, info, rows, fresh):
    count = blocks.shape[0]
    size = blocks.shape[1]
    n_dp = lax.axis_size("dp")
    n_mp = lax.axis_size("mp")
    for b in range(count):
        over_rep, over_mp, over_dp = b // (n_dp * n_mp), b // n_dp % n_mp, b % n_dp
        for t in range(3):
            line = blocks[b, size - 1 : size, t * 128 : (t + 1) * 128].astype(F32)
            rows[t : t + 1, b * size : (b + 1) * size] = line[:, :size]
            for m in range(n_mp):
                at = ((over_rep * n_dp + over_dp) * n_mp + (over_mp ^ m)) * new
                fresh[3 * m + t : 3 * m + t + 1, at : at + new] = line[:, size : size + new]
    label = rows[0:1, :]
    rank = rows[1:2, :] * 128.0 + rows[2:3, :]
    total = count * size
    info[0:1, :total] = label
    info[1:2, :total] = rank
    odd = jnp.full((1, 1), lax.axis_index("mp"), jnp.int32) == 1
    used = count * new
    info[0:1, total : total + used] = jnp.where(odd, fresh[3:4, :used], fresh[0:1, :used])
    info[1:2, total : total + used] = jnp.where(
        odd,
        fresh[4:5, :used] * 128.0 + fresh[5:6, :used],
        fresh[1:2, :used] * 128.0 + fresh[2:3, :used],
    )
    keys = jnp.concatenate([blocks[b] for b in range(count)], axis=0)
    similar = lax.dot_general(
        blocks[0], keys, (((1,), (1,)), ((), ())), preferred_element_type=F32
    )
    mine = labels[new:, :].astype(F32)
    at = ranks[new:, :].astype(F32)
    own = mine.shape[0]
    earlier = (label == mine) & (rank < at)
    best[:own, :] = jnp.max(jnp.where(earlier, similar[:own], -2.0), axis=1, keepdims=True)


def final_body(new, *refs):
    *sums, blocks, best, info, labels, ranks, out, pooled = refs
    docs = sums[0].shape[0] // (2 * len(sums))
    depth = sums[0].shape[1]
    n_dp = len(sums)
    for e in range(n_dp):
        for over_rep in range(2):
            for g in range(n_dp):
                source = (over_rep * n_dp + (e ^ g)) * docs
                at = (over_rep * n_dp + g) * docs
                pooled[at : at + docs, block_at(e, depth)] = sums[e][source : source + docs, :]
    units = unit_rows(pooled[...])
    count, size = blocks.shape[0], blocks.shape[1]
    total = count * size
    used = count * new
    keys = jnp.concatenate([blocks[b] for b in range(count)], axis=0)
    label, rank = info[0:1, :total], info[1:2, :total]
    new_label, new_rank = info[0:1, total : total + used], info[1:2, total : total + used]
    contract = (((1,), (1,)), ((), ()))
    similar = lax.dot_general(blocks[0], units, contract, preferred_element_type=F32)
    own = labels.shape[0] - new
    earlier = (new_label == labels[new:, :].astype(F32)) & (new_rank < ranks[new:, :].astype(F32))
    column = jnp.max(jnp.where(earlier, similar[:own], -2.0), axis=1, keepdims=True)
    column = jnp.maximum(column, best[:own, :])
    row = lax.broadcasted_iota(jnp.int32, (own, own + new), 0)
    lane = lax.broadcasted_iota(jnp.int32, (own, own + new), 1)
    result = jnp.sum(jnp.where(lane == row + new, column, 0.0), axis=0, keepdims=True)
    start = lax.axis_index("mp") * new
    row = lax.broadcasted_iota(jnp.int32, (8, 1), 0)
    mine = jnp.full((8, 1), -1.0, F32)
    place = jnp.zeros((8, 1), F32)
    for i in range(new):
        here = row == start + i
        mine = jnp.where(here, labels[i : i + 1, :].astype(F32), mine)
        place = jnp.where(here, ranks[i : i + 1, :].astype(F32), place)
    few = units[:8]
    similar = lax.dot_general(few, keys, contract, preferred_element_type=F32)
    column = jnp.max(
        jnp.where((label == mine) & (rank < place), similar, -2.0), axis=1, keepdims=True
    )
    similar = lax.dot_general(few, units, contract, preferred_element_type=F32)
    earlier = (new_label == mine) & (new_rank < place)
    column = jnp.maximum(
        column, jnp.max(jnp.where(earlier, similar, -2.0), axis=1, keepdims=True)
    )
    row = lax.broadcasted_iota(jnp.int32, (8, own + new), 0)
    lane = lax.broadcasted_iota(jnp.int32, (8, own + new), 1)
    inside = (lane == row - start) & (lane < new)
    result = result + jnp.sum(jnp.where(inside, column, 0.0), axis=0, keepdims=True)
    out[...] = jnp.where(result < -1.5, 0.0, result)


def fast(hidden_in, doc_lengths, w_qkv, w_out, w_up, w_down, stored_embed, doc_labels, doc_order):
    docs, seq, features = hidden_in.shape
    n_dp, n_mp, n_rep = lax.axis_size("dp"), lax.axis_size("mp"), lax.axis_size("rep")
    depth = w_qkv.shape[0]
    rows = docs * seq
    new = docs // n_mp
    index = [quarter_index(j) for j in range(QUARTERS)]

    qkv_local = jnp.transpose(w_qkv, (1, 0, 2))
    width = qkv_local.shape[2] // QUARTERS
    piece = lax.dynamic_slice_in_dim(qkv_local, index[0] * width, width, 2)
    qkv = [along_dp(piece)]
    out_peer = swap(w_out, "mp")
    qkv.append([swap(p, "rep") for p in qkv[0]])
    qkv.append([swap(p, "parts") for p in qkv[0]])
    qkv.append([swap(p, "rep") for p in qkv[2]])

    hidden = hidden_in.reshape(rows, features)
    normed = normalize(hidden.astype(F32)).astype(BF16)
    first = attention_call((0, 1), normed, qkv_local, qkv[0] + qkv[1], doc_lengths, docs)
    second = attention_call(
        (2, 3), after(normed, first), qkv_local, qkv[2] + qkv[3], doc_lengths, docs
    )

    out_rows = w_out.shape[0] // QUARTERS
    half = jnp.concatenate(
        [
            jnp.concatenate(
                [
                    lax.dynamic_slice_in_dim(w, index[j] * out_rows, out_rows, 0)
                    for w in (w_out, out_peer)
                ],
                axis=1,
            )
            for j in (0, 2)
        ],
        axis=0,
    )
    half = after(half, qkv[0][1])
    far = swap(half, "dp", 2)
    near = swap(half, "dp", 1)
    out_own = [near, far, swap(after(far, first), "dp", 1)]
    out_rep = [swap(after(p, first), "rep") for p in out_own]

    up_width = w_up.shape[1] // QUARTERS
    piece = lax.dynamic_slice_in_dim(w_up, index[0] * up_width, up_width, 1)
    piece = after(piece, first)
    up = [along_dp(piece)]
    ready = [after(p, second) for p in up[0]]
    up.append([swap(p, "rep") for p in ready])
    up.append([swap(p, "parts") for p in ready])
    up.append([swap(p, "rep") for p in up[2]])

    contexts = [first, second, swap(first, "mp"), swap(second, "mp")]
    hidden_normed, pooled = out_call(
        hidden, w_out, out_peer, contexts, out_own + out_rep, doc_lengths, docs
    )
    sums = up_call((0, 1), hidden_normed, w_up, up[0] + up[1], doc_lengths, docs)

    stored = stored_embed.shape[0]
    numbers = jnp.concatenate([doc_labels[:, 0], doc_order]).astype(jnp.int32)
    count = stored + new
    lane = jnp.arange(128, dtype=jnp.int32)

    def laid(values, filler):
        line = jnp.full((128,), filler, jnp.int32)
        line = lax.dynamic_update_slice(line, values[new:], (0,))
        return lax.dynamic_update_slice(line, values[:new], (stored + 1,))

    ranks = laid(numbers[count:], 0)
    last = jnp.concatenate([laid(numbers[:count], -1), ranks // 128, ranks % 128])
    last = jnp.pad(last, (0, features - last.shape[0])).astype(BF16)
    block = jnp.concatenate([unit_rows(stored_embed.astype(F32)), last[None, :]], axis=0)[None]
    block = after(block, second)
    every = jnp.concatenate([block, swap(block, "dp", 2)], axis=0)
    every = jnp.concatenate(
        [
            jnp.stack([a, b])
            for a, b in zip(every, swap(every, "dp", 1), strict=True)
        ],
        axis=0,
    )
    every = jnp.concatenate([every, swap(every, "mp")], axis=0)
    every = jnp.concatenate([every, swap(every, "rep")], axis=0)
    blocks = every.shape[0]
    order_column = doc_order[:, None]
    best, info = call(
        functools.partial(stored_body, new),
        [every, doc_labels, order_column],
        (
            jax.ShapeDtypeStruct((stored + 1, 1), F32),
            jax.ShapeDtypeStruct((2, blocks * (stored + 1) + 128), F32),
        ),
        [pltpu.VMEM((3, blocks * (stored + 1)), F32), pltpu.VMEM((3 * n_mp, 128), F32)],
        flops=2 * 64 * 1024 * 1024,
    )

    send = up_call(
        (2, 3), after(hidden_normed, sums), w_up, up[2] + up[3], doc_lengths, docs, (sums, pooled)
    )
    part = call(
        down_body,
        [send, *(swap(send, "dp", e) for e in range(1, n_dp)), w_down],
        jax.ShapeDtypeStruct((n_dp * docs, depth), F32),
        [pltpu.VMEM((n_dp * docs, send.shape[1]), F32)],
        flops=2 * 32 * 2048 * 256,
    )
    pair = call(
        sum_body,
        [part, swap(part, "mp"), swap(part, "rep"), both_swapped(part)],
        jax.ShapeDtypeStruct((n_rep * n_dp * docs, depth), F32),
    )
    result = call(
        functools.partial(final_body, new),
        [
            pair,
            *(swap(pair, "dp", e) for e in range(1, n_dp)),
            every,
            best,
            info,
            doc_labels,
            order_column,
        ],
        jax.ShapeDtypeStruct((1, stored + new), F32),
        [pltpu.VMEM((n_rep * n_dp * docs, features), F32)],
        flops=2 * 64 * 1024 * 1024,
    )
    return result[0]


def fits(mesh, hidden_in, w_qkv, w_out, w_up, stored_embed):
    size = mesh.shape
    depth = w_qkv.shape[0] // size["dp"]
    blocks = size["dp"] * size["mp"] * size["rep"] * size["parts"]
    return (
        size["parts"] == 2
        and size["rep"] == 2
        and size["mp"] == 2
        and size["dp"] == 4
        and depth % 128 == 0
        and w_qkv.shape[2] % (size["mp"] * 4 * 128) == 0
        and w_up.shape[1] % (size["mp"] * 4 * 128) == 0
        and size["mp"] * depth == w_up.shape[1] // (size["mp"] * 4)
        and hidden_in.shape[1] % 128 == 0
        and stored_embed.shape[0] // blocks == 63
    )


def solution(mesh):
    placed = (
        P(("parts", "dp", "rep"), None, None),
        P(("parts", "dp", "rep")),
        P("dp", None, "mp"),
        P("mp", "dp"),
        P("dp", "mp"),
        P("mp", "dp"),
        P(("parts", "dp", "mp", "rep"), None),
        P(("parts", "dp", "mp", "rep"), None),
        P(("parts", "dp", "mp", "rep")),
    )

    def run(*arrays):
        hidden_in, _, w_qkv, w_out, w_up, _, stored_embed = arrays[:7]
        plan = fast if fits(mesh, hidden_in, w_qkv, w_out, w_up, stored_embed) else shards
        return jax.shard_map(
            plan,
            mesh=mesh,
            in_specs=placed,
            out_specs=P(("parts", "dp", "mp", "rep")),
            check_vma=False,
        )(*arrays)

    return run
```
